32 devices in a mesh: section: 4 (over y, x), feat: 4 (over z), dp: 2 (over core).
Axes of the slice: x: 2, y: 2, z: 4, core: 2. Of those that a mesh axis runs over, the one named last changes fastest.
Arguments:
- section_outputs: bfloat16 [4, 1024, 4608], P('section', 'dp', 'feat'), may hold values from -6 to 6
- enc_weight: bfloat16 [4608, 16384], P('dp', ('section', 'feat')), may hold values from -0.09375 to 0.09375
- enc_bias: float32 [16384], P(('section', 'feat')), may hold values from -3 to 3
- thresholds: int32 [16384], P(('section', 'feat')), may hold values from 0 to 7
- dec_weight: bfloat16 [16384, 4608], P(('section', 'feat'), 'dp'), may hold values from -0.09375 to 0.09375
- dec_bias: float32 [4608], replicated, may hold values from -3 to 3
- enc_moment: float32 [4608, 16384], P('dp', ('section', 'feat')), may hold values from -2 to 2
- enc_second: float32 [4608, 16384], P('dp', ('section', 'feat')), may hold values from 0.01 to 1
- dec_moment: float32 [16384, 4608], P(('section', 'feat'), 'dp'), may hold values from -2 to 2
- dec_second: float32 [16384, 4608], P(('section', 'feat'), 'dp'), may hold values from 0.01 to 1
Outputs:
- enc_update: bfloat16 [4608, 16384], P('dp', ('section', 'feat'))
- enc_moment_new: float32 [4608, 16384], P('dp', ('section', 'feat'))
- enc_second_new: float32 [4608, 16384], P('dp', ('section', 'feat'))
- dec_update: bfloat16 [16384, 4608], P(('section', 'feat'), 'dp')
- dec_moment_new: float32 [16384, 4608], P(('section', 'feat'), 'dp')
- dec_second_new: float32 [16384, 4608], P(('section', 'feat'), 'dp')
The draws below stay inside these ranges and needn't reach their ends.
All inputs are finite; a program needn't handle non-finite values.
Results may differ from the reference program's by a relative error of at most 0.0055.
The reference program's roundings to bfloat16 on the way (of `resid`, `codes`, `grad_out` and `pre_grad`) count: a program that leaves them out, or rounds other values in their place, can miss the bound.
Values may be sent and summed in bfloat16 or wider, within the bound.
No kernel may reach another device: no remote copies, remote signals or barrier semaphores. Data moves between devices by JAX's collectives and lax.ppermute only.
A program may use at most 256 MiB of HBM per device.

```python
import math
import jax
import jax.numpy as jnp
from jax import lax

D = 4608
F = 16384
TOKENS = 1024
SECTIONS = 4


def touch_ends(entries, rng, least, top_value):
    longest = entries.shape.index(max(entries.shape))
    spots = []
    for shift in (0, 1):
        where = [jax.random.randint(jax.random.fold_in(rng, axis), (), 0, length) for axis, length in enumerate(entries.shape)]
        where[longest] = (where[longest] + shift) % entries.shape[longest]
        spots.append(tuple(where))
    return entries.at[spots[0]].set(least).at[spots[1]].set(top_value)


def block_scale(own_key, shape, pieces, low, top_value):
    level, own = 1.0, jax.random.fold_in(own_key, 6)
    for position, blocks in pieces:
        draws = jnp.exp(jax.random.uniform(jax.random.fold_in(own, position), (blocks,), jnp.float32, low / len(pieces), top_value / len(pieces)))
        level = level * jnp.repeat(draws, shape[position] // blocks).reshape([-1 if axis == position else 1 for axis in range(len(shape))])
    return level


def scatter_about(own_key, shape, scale, most, split=(), dtype=jnp.bfloat16):
    entries = scale * jax.random.normal(own_key, shape, jnp.float32)
    if split:
        entries = entries * block_scale(own_key, shape, split, -0.22, 0.18)
    return jnp.clip(entries, -most, most).astype(dtype)


def setup_inputs(seed: int = 0) -> dict:
    seeds = jax.random.split(jax.random.key(seed), 11)
    section_outputs = scatter_about(seeds[0], (SECTIONS, TOKENS, D), 1.0, 6.0, ((0, 4), (1, 2), (2, 4)))
    enc_weight = scatter_about(seeds[1], (D, F), D ** -0.5, 0.09375, ((0, 2), (1, 16)))
    enc_bias = scatter_about(seeds[2], (F,), 0.5, 3.0, ((0, 16),), jnp.float32)
    thresholds = touch_ends(jax.random.randint(seeds[3], (F,), 0, 8), jax.random.fold_in(seeds[3], 1), 0, 7).astype(jnp.int32)
    dec_weight = scatter_about(seeds[4], (F, D), (F // 4) ** -0.5, 0.09375, ((0, 16), (1, 2)))
    dec_bias = scatter_about(seeds[5], (D,), 0.5, 3.0, (), jnp.float32)
    enc_moment = scatter_about(seeds[6], (D, F), 0.3, 2.0, ((0, 2), (1, 16)), jnp.float32)
    enc_second = jnp.clip(jnp.exp(math.log(1.0) - 4.6051702 * jax.random.uniform(seeds[7], (D, F), jnp.float32) ** block_scale(seeds[7], (D, F), ((0, 2), (1, 16)), -0.2, 0.2)), 0.01, 1.0)
    dec_moment = scatter_about(seeds[8], (F, D), 0.3, 2.0, ((0, 16), (1, 2)), jnp.float32)
    dec_second = jnp.clip(jnp.exp(math.log(1.0) - 4.6051702 * jax.random.uniform(seeds[9], (F, D), jnp.float32) ** block_scale(seeds[9], (F, D), ((0, 16), (1, 2)), -0.2, 0.2)), 0.01, 1.0)
    return {"section_outputs": section_outputs, "enc_weight": enc_weight, "enc_bias": enc_bias, "thresholds": thresholds, "dec_weight": dec_weight, "dec_bias": dec_bias, "enc_moment": enc_moment, "enc_second": enc_second, "dec_moment": dec_moment, "dec_second": dec_second}


band = 0.1
level_step = 0.25
beta_first = 0.9
beta_second = 0.999
fix_first = 1.0 - (0.9 ** 50) ** 2
fix_second = 1.0 - (0.999 ** 50) ** 2
epsilon = 1e-08

def adam_moves(moment, second, grads):
    moment_new = beta_first * moment + (1.0 - beta_first) * grads
    second_new = beta_second * second + (1.0 - beta_second) * grads * grads
    update = (moment_new / fix_first / (jnp.sqrt(second_new / fix_second) + epsilon)).astype(jnp.bfloat16)
    return (update, moment_new, second_new)

def reference(section_outputs, enc_weight, enc_bias, thresholds, dec_weight, dec_bias, enc_moment, enc_second, dec_moment, dec_second):
    resid = lax.optimization_barrier(jnp.sum(section_outputs.astype(jnp.float32), axis=0)).astype(jnp.bfloat16)
    preact = jnp.dot(resid, enc_weight, preferred_element_type=jnp.float32) + enc_bias
    theta = level_step * (thresholds.astype(jnp.float32) + 1.0)
    opened = jax.nn.sigmoid((preact - theta) / band)
    codes = (preact * opened).astype(jnp.bfloat16)
    recon = jnp.dot(codes, dec_weight, preferred_element_type=jnp.float32) + dec_bias
    grad_out = ((recon - resid.astype(jnp.float32)) / math.sqrt(TOKENS)).astype(jnp.bfloat16)
    dec_grad = jax.lax.dot_general(codes, grad_out, (((0,), (0,)), ((), ())), preferred_element_type=jnp.float32)
    back = jax.lax.dot_general(grad_out, dec_weight, (((1,), (1,)), ((), ())), preferred_element_type=jnp.float32)
    pre_grad = (back * (opened + preact * opened * (1.0 - opened) / band)).astype(jnp.bfloat16)
    enc_grad = jax.lax.dot_general(resid, pre_grad, (((0,), (0,)), ((), ())), preferred_element_type=jnp.float32)
    enc_update, enc_moment_new, enc_second_new = adam_moves(enc_moment, enc_second, enc_grad)
    dec_update, dec_moment_new, dec_second_new = adam_moves(dec_moment, dec_second, dec_grad)
    return (enc_update, enc_moment_new, enc_second_new, dec_update, dec_moment_new, dec_second_new)
```

```python
import math

import jax
import jax.numpy as jnp
from jax import lax
from jax.sharding import PartitionSpec as P


band = 0.1
level_step = 0.25
beta_first = 0.9
beta_second = 0.999
fix_first = 1.0 - (0.9**50) ** 2
fix_second = 1.0 - (0.999**50) ** 2
epsilon = 1e-08
halves = 2
direct_limit = 8


def adam_moves(moment, second, grads):
    moment_new = beta_first * moment + (1.0 - beta_first) * grads
    second_new = beta_second * second + (1.0 - beta_second) * grads * grads
    update = (moment_new / fix_first / (jnp.sqrt(second_new / fix_second) + epsilon)).astype(
        jnp.bfloat16
    )
    return (update, moment_new, second_new)


def swap(value, axis, mask):
    size = lax.axis_size(axis)
    return lax.ppermute(value, axis, [(place, place ^ mask) for place in range(size)])


def gather_columns(piece):
    size = lax.axis_size("feat")
    place = lax.axis_index("feat")
    turn = lax.axis_index("dp") * (size // lax.axis_size("dp"))
    rows, width = piece.shape
    if size > direct_limit:
        whole = lax.all_gather(piece, "feat", axis=1, tiled=True)
        return jnp.where(turn == 0, whole, jnp.roll(whole, width * size // 2, axis=1))
    joined = jnp.zeros((rows, width * size), piece.dtype)
    for mask in range(size):
        block = swap(piece, "feat", mask) if mask else piece
        spot = lax.rem((place ^ mask) + turn, size) * width
        joined = lax.dynamic_update_slice(joined, block, (0, spot))
    return joined


def scatter_columns(sums):
    size = lax.axis_size("feat")
    place = lax.axis_index("feat")
    turn = lax.axis_index("dp") * (size // lax.axis_size("dp"))
    rows, whole = sums.shape
    width = whole // size
    if size > direct_limit:
        sums = jnp.where(turn == 0, sums, jnp.roll(sums, whole // 2, axis=1))
        return lax.psum_scatter(sums, "feat", scatter_dimension=1, tiled=True)
    total = None
    for mask in range(size):
        spot = lax.rem((place ^ mask) + turn, size) * width
        block = lax.dynamic_slice(sums, (0, spot), (rows, width))
        if mask:
            block = swap(block.astype(jnp.bfloat16), "feat", mask).astype(jnp.float32)
        total = block if total is None else total + block
    return total


def bit_orders(size):
    bits = [1 << place for place in range(size.bit_length() - 1)]
    return [bits[turn:] + bits[:turn] for turn in range(len(bits))] or [[]]


def gather_rows(part, order):
    blocks = {0: part}
    for bit in order:
        for mask in list(blocks):
            blocks[mask | bit] = swap(blocks[mask], "section", bit)
    return blocks


def scatter_rows(blocks, order):
    blocks = {mask: block.astype(jnp.float32) for mask, block in blocks.items()}
    for bit in reversed(order):
        for mask in [mask for mask in blocks if mask & bit]:
            moved = swap(blocks.pop(mask).astype(jnp.bfloat16), "section", bit)
            blocks[mask ^ bit] = blocks[mask ^ bit] + moved.astype(jnp.float32)
    return blocks[0]


def spread(piece, orders):
    wide = gather_columns(piece)
    step = wide.shape[0] // len(orders)
    parts = [
        gather_rows(wide[turn * step : (turn + 1) * step], order)
        for turn, order in enumerate(orders)
    ]
    return jnp.concatenate(
        [part[mask] for mask in range(lax.axis_size("section")) for part in parts], axis=0
    )


def collect(partial, orders):
    sections = lax.axis_size("section")
    step = partial.shape[0] // sections // len(orders)
    sums = []
    for turn, order in enumerate(orders):
        blocks = {}
        for mask in range(sections):
            first = (mask * len(orders) + turn) * step
            blocks[mask] = partial[first : first + step]
        sums.append(scatter_rows(blocks, order))
    return scatter_columns(jnp.concatenate(sums, axis=0))


def on_device(
    section_outputs,
    enc_weight,
    enc_bias,
    thresholds,
    dec_weight,
    dec_bias,
    enc_moment,
    enc_second,
    dec_moment,
    dec_second,
):
    sections = lax.axis_size("section")
    own = lax.axis_index("section")
    tok_rows, width = section_outputs.shape[1:]
    token_total = tok_rows * lax.axis_size("dp")
    rows = tok_rows // sections
    half_rows = rows // halves
    half_width = enc_weight.shape[0]
    orders = bit_orders(sections)

    enc_full = jnp.concatenate([enc_weight, swap(enc_weight, "dp", 1)], axis=0)
    dec_full = jnp.concatenate([dec_weight, swap(dec_weight, "dp", 1)], axis=1)
    theta = level_step * (thresholds.astype(jnp.float32) + 1.0)
    bias_part = lax.dynamic_slice_in_dim(dec_bias, lax.axis_index("feat") * width, width, 0)

    pieces = []
    for half in range(halves):
        total = None
        for mask in range(sections):
            first = (own ^ mask) * rows + half * half_rows
            block = lax.dynamic_slice(section_outputs[0], (first, 0), (half_rows, width))
            if mask:
                block = swap(block, "section", mask)
            block = block.astype(jnp.float32)
            total = block if total is None else total + block
        pieces.append(total.astype(jnp.bfloat16))

    resid, preact, codes, grad_out = [], [], [], []
    for half in range(halves):
        resid.append(spread(pieces[half], orders))
        preact.append(
            jnp.dot(resid[half], enc_full, preferred_element_type=jnp.float32) + enc_bias
        )
        opened = jax.nn.sigmoid((preact[half] - theta) / band)
        codes.append((preact[half] * opened).astype(jnp.bfloat16))
        partial = jnp.dot(codes[half], dec_full, preferred_element_type=jnp.float32)
        recon = collect(partial.astype(jnp.bfloat16), orders)
        error_part = (recon + bias_part - pieces[half].astype(jnp.float32)) / math.sqrt(
            token_total
        )
        grad_out.append(spread(error_part.astype(jnp.bfloat16), orders))

    pre_grad = []
    for half in range(halves):
        back = lax.dot_general(
            grad_out[half], dec_full, (((1,), (1,)), ((), ())), preferred_element_type=jnp.float32
        )
        opened = jax.nn.sigmoid((preact[half] - theta) / band)
        pre_grad.append(
            (back * (opened + preact[half] * opened * (1.0 - opened) / band)).astype(jnp.bfloat16)
        )

    def both(parts):
        return jnp.concatenate(parts + [swap(part, "dp", 1) for part in parts], axis=0)

    def both_halves(parts):
        return jnp.concatenate(
            [part[:, :half_width] for part in parts]
            + [swap(part[:, half_width:], "dp", 1) for part in parts],
            axis=0,
        )

    over_rows = (((0,), (0,)), ((), ()))
    dec_grad = lax.dot_general(
        both(codes), both_halves(grad_out), over_rows, preferred_element_type=jnp.float32
    )
    dec_update, dec_moment_new, dec_second_new = adam_moves(dec_moment, dec_second, dec_grad)
    enc_grad = lax.dot_general(
        both_halves(resid), both(pre_grad), over_rows, preferred_element_type=jnp.float32
    )
    enc_update, enc_moment_new, enc_second_new = adam_moves(enc_moment, enc_second, enc_grad)
    return (enc_update, enc_moment_new, enc_second_new, dec_update, dec_moment_new, dec_second_new)


def solution(mesh):
    return jax.shard_map(
        on_device,
        mesh=mesh,
        in_specs=(
            P("section", "dp", "feat"),
            P("dp", ("section", "feat")),
            P(("section", "feat")),
            P(("section", "feat")),
            P(("section", "feat"), "dp"),
            P(),
            P("dp", ("section", "feat")),
            P("dp", ("section", "feat")),
            P(("section", "feat"), "dp"),
            P(("section", "feat"), "dp"),
        ),
        out_specs=(
            P("dp", ("section", "feat")),
            P("dp", ("section", "feat")),
            P("dp", ("section", "feat")),
            P(("section", "feat"), "dp"),
            P(("section", "feat"), "dp"),
            P(("section", "feat"), "dp"),
        ),
        check_vma=False,
    )
```
